512 devices in a mesh: chrom: 8 (over x, y_hi), samp: 64 (over z, y_lo, core).
Axes of the slice: x: 4, y: 8 (y_hi: 2, y_lo: 4; y = y_hi * 4 + y_lo), z: 8, core: 2. Of those that a mesh axis runs over, the one named last changes fastest.
Arguments:
- genotypes: int32 [24576, 24576], P('samp', 'chrom'), may hold values from 0 to 2, as said below
- frequency: float32 [24576], P('chrom'), may hold values from 0.05 to 0.5, as said below
- widths: int32 [8], replicated, may hold values from 1 to 6144, 24576 in all
- ridge_term: float32 [1], replicated, may hold values from 0.5 to 1.5
- direction: float32 [24576, 64], P('samp'), may hold values from -6 to 6
Outputs:
- loco_out: float32 [8, 24576, 64], P('chrom', 'samp')
The draws below stay inside these ranges and needn't reach their ends.
Inputs may be any that keep to these rules, and one draw needn't show every extreme that they name: Each variant's allele frequency is a whole number of thousandths. `genotypes`: each dosage, apart from samples 0 and 1 at variant 0 (set to 2 and 0), is the sum of two independent draws that are 1 with the variant's allele frequency and 0 otherwise. The 8 widths sum to 24576.
All inputs are finite; a program needn't handle non-finite values.
Results may differ from the reference program's by a relative error of at most 0.004.
Values may be sent and summed in bfloat16 or wider, within the bound.
A program may use at most 64 MiB of HBM per device.

```python
import math
import jax
import jax.numpy as jnp
import numpy as np
from jax import lax

VAR_DEV = 3072
K = 64
SECTIONS = 8
SAMPLES = 24576
VARIANTS = 24576
N_CHROM = 8


def thousandths(key):
    return jax.random.randint(jax.random.fold_in(key, 7301), (VARIANTS,), 50, 501).astype(jnp.int32)


def draw_frequency(key, part):
    return (thousandths(key).astype(jnp.float32) / 1000.0).astype(jnp.float32)


def draw_genotypes(key, part):
    levels = thousandths(key)
    first = jax.random.randint(jax.random.fold_in(key, 7302), (SAMPLES, VARIANTS), 0, 1000)
    second = jax.random.randint(jax.random.fold_in(key, 7303), (SAMPLES, VARIANTS), 0, 1000)
    dosage = (first < levels[None, :]).astype(jnp.int32) + (second < levels[None, :]).astype(jnp.int32)
    dosage = dosage.at[0, 0].set(2)
    dosage = dosage.at[1, 0].set(0)
    return dosage.astype(jnp.int32)


def steps_of(stream_key, shape, pieces, least, top_value):
    def one(dim, shards_of):
        heights = jax.random.uniform(jax.random.fold_in(jax.random.fold_in(stream_key, 6), dim), (shards_of,), jnp.float32, least / len(pieces), top_value / len(pieces))
        return jnp.repeat(jnp.exp(heights), shape[dim] // shards_of).reshape((-1,) + (1,) * (len(shape) - dim - 1))

    loudness = one(*pieces[0])
    for cut in pieces[1:]:
        loudness = loudness * one(*cut)
    return loudness


def length_profile(number_of, total, most, lean):
    portions = [(1 << 20) // math.isqrt(grade ** lean) + 1 for grade in range(2, number_of + 1)]
    rest, counts = total - most - (number_of - 1), [1] * (number_of - 1)
    while rest > 0:
        candidates = [i for i in range(number_of - 1) if counts[i] < most]
        mass, budget = sum([portions[i] for i in candidates]), rest
        for i in candidates:
            addition = min(most - counts[i], max(1, budget * portions[i] // mass), rest)
            counts[i] = counts[i] + addition
            rest = rest - addition
    return np.array([most] + counts)


def ragged(key, count, total, most, lean):
    if count == 2:
        one = jax.random.randint(key, (), max(1, total - most), min(most, total - 1) + 1)
        return jnp.stack([one, total - one])
    lengths = jnp.asarray(length_profile(count, total, most, lean), jnp.int32)
    couples = (count - 1) // 2
    giver, receiver = lengths[1:1 + 2 * couples:2], lengths[2:2 + 2 * couples:2]
    slack = jnp.minimum(giver - 1, most - receiver)
    passed = jax.random.randint(jax.random.fold_in(key, 1), (couples,), 0, 1 << 20) % (slack + 1)
    lengths = lengths.at[1:1 + 2 * couples:2].set(giver - passed).at[2:2 + 2 * couples:2].set(receiver + passed)
    return lengths[jax.random.permutation(jax.random.fold_in(key, 2), count)]


def scatter_about(rng, extent, scale, bound, shards=(), kind=jnp.bfloat16):
    entries = jax.random.normal(rng, extent, jnp.float32) * scale
    if len(shards) > 0:
        entries = steps_of(rng, extent, shards, -0.22, 0.18) * entries
    return jnp.clip(entries, min=-bound, max=bound).astype(kind)


def setup_inputs(seed: int = 0) -> dict:
    seeds = jax.random.split(jax.random.key(seed), 6)
    return {
        "genotypes": draw_genotypes(jax.random.fold_in(seeds[5], 71), 0),
        "frequency": draw_frequency(jax.random.fold_in(seeds[5], 71), 0),
        "widths": ragged(seeds[2], SECTIONS, VARIANTS, VARIANTS // 4, 2).astype(jnp.int32),
        "ridge_term": jnp.clip(jax.random.uniform(seeds[3], (1,), jnp.float32, 0.5, 1.5), 0.5, 1.5),
        "direction": scatter_about(seeds[4], (SAMPLES, K), 1.0, 6.0, ((0, 64),), jnp.float32),
    }


def reference(genotypes, frequency, widths, ridge_term, direction):
    vector = lax.optimization_barrier(direction.astype(jnp.bfloat16)).astype(jnp.float32)
    section_ends = jnp.cumsum(widths).astype(jnp.int32)
    labels = jnp.arange(SECTIONS, dtype=jnp.int32)

    def one_block(running, block_index):
        offset = (block_index * VAR_DEV).astype(jnp.int32)
        dosage = lax.dynamic_slice_in_dim(genotypes, offset, VAR_DEV, 1)
        allele_freq = lax.dynamic_slice_in_dim(frequency, offset, VAR_DEV, 0)
        doubled = 2.0 * allele_freq
        standard = ((dosage.astype(jnp.float32) - doubled) * lax.rsqrt(doubled * (1.0 - allele_freq))).astype(jnp.bfloat16)
        standard = lax.optimization_barrier(standard).astype(jnp.float32)
        crossed = jnp.dot(standard.T, vector, precision=lax.Precision.HIGHEST)
        shared = lax.optimization_barrier(crossed.astype(jnp.bfloat16)).astype(jnp.float32)
        var_index = offset + jnp.arange(VAR_DEV, dtype=jnp.int32)
        section = lax.optimization_barrier(jnp.sum((var_index[:, None] >= section_ends[None, :]).astype(jnp.int32), axis=1))
        onehot = (section[:, None] == labels[None, :]).astype(jnp.float32)
        spread = (shared[:, None, :] * onehot[:, :, None]).reshape(VAR_DEV, SECTIONS * K)
        return (running + jnp.dot(standard, spread, precision=lax.Precision.HIGHEST), None)
    initial = jnp.zeros((SAMPLES, SECTIONS * K), jnp.float32)
    partial_value, _ = lax.scan(one_block, initial, jnp.arange(N_CHROM, dtype=jnp.int32))
    by_section = partial_value.reshape(SAMPLES, SECTIONS, K)
    all_total = lax.optimization_barrier(jnp.sum(by_section, axis=1))
    divisor = (VARIANTS - widths).astype(jnp.float32)
    own_sums = jnp.transpose(by_section, (1, 0, 2))
    return ridge_term[0] * direction[None, :, :] + (all_total[None, :, :] - own_sums) / divisor[:, None, None]
```

```python
import jax
import jax.numpy as jnp
from jax import lax
from jax.experimental import pallas as pl
from jax.experimental.pallas import tpu as pltpu
from jax.sharding import PartitionSpec as P

MESH = pl.DeviceIdType.MESH
NZ, NY, NCORE = 8, 4, 2
NX, NH = 4, 2
BF16, F32 = jnp.bfloat16, jnp.float32


def far_first(i):
    half = NZ // 2
    return lax.rem(jnp.where(lax.rem(i, 2) == 1, half + (i + 1) // 2, half - i // 2), NZ)


def near_first(i):
    return lax.rem(jnp.where(lax.rem(i, 2) == 1, (i + 1) // 2, NZ - i // 2), NZ)


def kernel(
    gen_hbm, freq_ref, widths_ref, ridge_ref, dir_ref, out_ref,
    gbuf, std, own, psend, precv, rsend, rrecv, shared, acc, xsend, xrecv, ysend, yrecv, bounds,
    gsem, psend_sem, precv_sem, rsend_sem, rrecv_sem, asend_sem, arecv_sem, fsend_sem, frecv_sem,
    xsend_sem, xrecv_sem, ysend_sem, yrecv_sem,
):
    rhs, rows = dir_ref.shape
    group = gbuf.shape[2]
    variants = NX * NH * NZ * group
    ci, si = lax.axis_index("chrom"), lax.axis_index("samp")
    z, y, core = si // (NY * NCORE), lax.rem(si // NCORE, NY), lax.rem(si, NCORE)
    x, yh = ci // NH, lax.rem(ci, NH)

    def samp_dev(off, dq):
        return (ci, (lax.rem(z + off, NZ) * NY + lax.rem(y + dq, NY)) * NCORE + core)

    partner = (ci, si + 1 - 2 * core)

    def chrom_dev(dx, dh):
        return (lax.rem(x + dx, NX) * NH + lax.rem(yh + dh, NH), si)

    def lane_group(off):
        return lax.rem(z + off, NZ)

    def gcopy(i):
        lanes = pl.ds(pl.multiple_of(lane_group(far_first(i)) * group, 128), group)
        return pltpu.make_async_copy(gen_hbm.at[:, lanes], gbuf.at[i], gsem.at[i])

    def start_gcopy(i, _):
        gcopy(i).start()
        return 0

    lax.fori_loop(0, NZ, start_gcopy, 0)

    barrier = pltpu.get_barrier_semaphore()
    peers = 0
    for off in (4, 5, 3, 6, 2, 7, 1, 0):
        for dq in range(NY):
            if off or dq:
                pl.semaphore_signal(barrier, inc=1, device_id=samp_dev(off, dq), device_id_type=MESH)
                peers += 1
    for dx, dh in ((0, 1), (2, 0), (1, 0), (3, 0)):
        pl.semaphore_signal(barrier, inc=1, device_id=chrom_dev(dx, dh), device_id_type=MESH)
        peers += 1
    pl.semaphore_signal(barrier, inc=1, device_id=partner, device_id_type=MESH)
    peers += 1

    total = jnp.int32(0)
    for c in range(NX * NH):
        bounds[0, c] = total
        total = total + widths_ref[c]
        bounds[1, c] = total

    vector = dir_ref[...].astype(BF16)

    def first_products(i, _):
        gcopy(i).wait()
        lg = lane_group(far_first(i))
        freq = freq_ref[:, pl.ds(pl.multiple_of(lg * group, 128), group)]
        doubled = 2.0 * freq
        scale = lax.rsqrt(doubled * (1.0 - freq))
        block = ((gbuf[i].astype(F32) - doubled) * scale).astype(BF16)
        std[lg] = block
        own[i] = jnp.dot(vector, block, preferred_element_type=F32)
        return 0

    lax.fori_loop(0, NZ, first_products, 0)

    pl.semaphore_wait(barrier, peers)

    half = rhs // NCORE

    def pair_copy(i):
        return pltpu.make_async_remote_copy(
            src_ref=psend.at[i], dst_ref=precv.at[i],
            send_sem=psend_sem.at[i], recv_sem=precv_sem.at[i],
            device_id=partner, device_id_type=MESH,
        )

    def pair_start(i, _):
        theirs = pl.multiple_of((1 - core) * half, half)
        psend[i] = own[i, pl.ds(theirs, half), :].astype(BF16)
        pair_copy(i).start()
        return 0

    lax.fori_loop(0, NZ, pair_start, 0)

    def scatter_copy(i, off, dq):
        return pltpu.make_async_remote_copy(
            src_ref=rsend.at[i, lax.rem(y + dq, NY)], dst_ref=rrecv.at[off, dq],
            send_sem=rsend_sem, recv_sem=rrecv_sem.at[off],
            device_id=samp_dev(off, dq), device_id_type=MESH,
        )

    def pair_sum(i):
        pair_copy(i).wait()
        mine = pl.multiple_of(core * half, half)
        value = own[i, pl.ds(mine, half), :] + precv[i].astype(F32)
        rsend[i] = value.astype(BF16).reshape(NY, half // NY, group)

    def scatter(i, _):
        pair_sum(i)
        off = far_first(i)
        for dq in (2, 3, 1, 0):
            scatter_copy(i, off, dq).start()
        return 0

    lax.fori_loop(0, NZ - 1, scatter, 0)
    pair_sum(NZ - 1)
    for dq in range(1, NY):
        scatter_copy(NZ - 1, 0, dq).start()

    block = rsend[NZ - 1, y].astype(F32)
    for off in (0, 1, 7, 2, 6, 3, 5, 4):
        part = rrecv.at[off, pl.ds(1, NY - 1)] if off == 0 else rrecv.at[off]
        pltpu.make_async_copy(part, part, rrecv_sem.at[off]).wait()
        for dq in range(NY):
            if off or dq:
                block = block + rrecv[off, dq].astype(F32)
    shared[z, core, y] = block.astype(BF16)

    def gather_copy(off, dq):
        return pltpu.make_async_remote_copy(
            src_ref=shared.at[z, core, y], dst_ref=shared.at[z, core, y],
            send_sem=asend_sem, recv_sem=arecv_sem.at[off],
            device_id=samp_dev(off, dq), device_id_type=MESH,
        )

    def gather(i, _):
        for dq in (2, 3, 1, 0):
            gather_copy(far_first(i), dq).start()
        return 0

    lax.fori_loop(0, NZ - 1, gather, 0)
    for dq in range(1, NY):
        gather_copy(0, dq).start()

    def forward_copy(off):
        lg = lax.rem(z + NZ - off, NZ)
        return pltpu.make_async_remote_copy(
            src_ref=shared.at[lg, core], dst_ref=shared.at[lg, core],
            send_sem=fsend_sem, recv_sem=frecv_sem.at[off],
            device_id=partner, device_id_type=MESH,
        )

    part = rrecv.at[0, pl.ds(1, NY - 1)]
    pltpu.make_async_copy(part, part, arecv_sem.at[0]).wait()
    forward_copy(0).start()

    def forward(i, _):
        off = near_first(i)
        pltpu.make_async_copy(rrecv.at[0], rrecv.at[0], arecv_sem.at[off]).wait()
        forward_copy(off).start()
        return 0

    lax.fori_loop(1, NZ, forward, 0)

    acc[...] = jnp.zeros_like(acc)
    order = [(dx, dh) for dh in (1, 0) for dx in (2, 1, 3, 0)]
    sections = [lax.rem(x + dx, NX) * NH + lax.rem(yh + dh, NH) for dx, dh in order]

    def second_products(i, _):
        off = near_first(i)
        lg = lax.rem(z + NZ - off, NZ)
        forward_copy(off).wait_recv()
        value = shared[lg].astype(F32).reshape(rhs, group)
        var = (ci * NZ + lg) * group + lax.broadcasted_iota(jnp.int32, (1, group), 1)
        pieces = []
        for c in sections:
            inside = (var >= bounds[0, c]) & (var < bounds[1, c])
            pieces.append((value * jnp.where(inside, 0.0, 1.0)).astype(BF16))
        lhs = jnp.concatenate(pieces, axis=0)
        acc[...] += lax.dot_general(
            lhs, std[lg], (((1,), (1,)), ((), ())), preferred_element_type=F32
        )
        return 0

    lax.fori_loop(0, NZ, second_products, 0)

    def x_copy(j, dx, dh):
        return pltpu.make_async_remote_copy(
            src_ref=xsend.at[j], dst_ref=xrecv.at[j],
            send_sem=xsend_sem.at[j], recv_sem=xrecv_sem.at[j],
            device_id=chrom_dev(dx, 0), device_id_type=MESH,
        )

    for j, (dx, dh) in enumerate(order):
        if dx:
            xsend[j] = acc[j * rhs : (j + 1) * rhs, :].astype(BF16)
            x_copy(j, dx, dh).start()

    def x_sum(first):
        value = acc[(first + NX - 1) * rhs : (first + NX) * rhs, :]
        for j in range(first, first + NX - 1):
            x_copy(j, *order[j]).wait()
            value = value + xrecv[j].astype(F32)
        return value

    ysend[...] = x_sum(0).astype(BF16)
    y_copy = pltpu.make_async_remote_copy(
        src_ref=ysend, dst_ref=yrecv, send_sem=ysend_sem, recv_sem=yrecv_sem,
        device_id=chrom_dev(0, 1), device_id_type=MESH,
    )
    y_copy.start()
    mine = x_sum(NX)
    divisor = (variants - widths_ref[ci]).astype(F32)
    y_copy.wait()
    out_ref[...] = ridge_ref[0] * dir_ref[...] + (mine + yrecv[...].astype(F32)) / divisor

    sent = rrecv.at[pl.ds(1, NZ - 1)]
    rest = rrecv.at[0, pl.ds(1, NY - 1)]
    for sem in (rsend_sem, asend_sem):
        pltpu.make_async_copy(sent, sent, sem).wait()
        pltpu.make_async_copy(rest, rest, sem).wait()
    whole = shared.at[:, 0]
    pltpu.make_async_copy(whole, whole, fsend_sem).wait()


def on_device(genotypes, frequency, widths, ridge_term, direction):
    rows, local_vars = genotypes.shape
    rhs = direction.shape[1]
    group = local_vars // NZ
    half = rhs // NCORE
    piece = half // NY
    sections = NX * NH
    dma, regular = pltpu.SemaphoreType.DMA, pltpu.SemaphoreType.REGULAR
    vmem, smem = pltpu.VMEM, pltpu.SMEM
    out = pl.pallas_call(
        kernel,
        out_shape=jax.ShapeDtypeStruct((rhs, rows), F32),
        in_specs=[
            pl.BlockSpec(memory_space=pl.ANY),
            pl.BlockSpec(memory_space=vmem),
            pl.BlockSpec(memory_space=smem),
            pl.BlockSpec(memory_space=smem),
            pl.BlockSpec(memory_space=vmem),
        ],
        out_specs=pl.BlockSpec(memory_space=vmem),
        scratch_shapes=[
            vmem((NZ, rows, group), jnp.int32),
            vmem((NZ, rows, group), BF16),
            vmem((NZ, rhs, group), F32),
            vmem((NZ, half, group), BF16),
            vmem((NZ, half, group), BF16),
            vmem((NZ, NY, piece, group), BF16),
            vmem((NZ, NY, piece, group), BF16),
            vmem((NZ, NCORE, NY, piece, group), BF16),
            vmem((sections * rhs, rows), F32),
            vmem((sections, rhs, rows), BF16),
            vmem((sections, rhs, rows), BF16),
            vmem((rhs, rows), BF16),
            vmem((rhs, rows), BF16),
            smem((2, sections), jnp.int32),
            dma((NZ,)), dma((NZ,)), dma((NZ,)),
            dma, dma((NZ,)), dma, dma((NZ,)), dma, dma((NZ,)),
            dma((sections,)), dma((sections,)), dma, dma,
        ],
        compiler_params=pltpu.CompilerParams(collective_id=0, has_side_effects=True),
        name="loco",
    )(genotypes, frequency.reshape(1, local_vars), widths, ridge_term, direction.T)
    return out.T[None]


def solution(mesh):
    return jax.shard_map(
        on_device,
        mesh=mesh,
        in_specs=(P("samp", "chrom"), P("chrom"), P(), P(), P("samp", None)),
        out_specs=P("chrom", "samp", None),
        check_vma=False,
    )
```

```python
import jax
import jax.numpy as jnp
from jax import lax
from jax.experimental import pallas as pl
from jax.experimental.pallas import tpu as pltpu
from jax.sharding import PartitionSpec as P

MESH = pl.DeviceIdType.MESH
NZ, NY, NCORE = 8, 4, 2
NX, NH = 4, 2
CHUNKS = ((0, 8),)
BF16, F32 = jnp.bfloat16, jnp.float32


def loop(start, stop, body, carry):
    for i in range(start, stop):
        body(i, carry)


def far_first(i):
    half = NZ // 2
    return (half + (i + 1) // 2 if i % 2 else half - i // 2) % NZ


def near_first(i):
    return ((i + 1) // 2 if i % 2 else NZ - i // 2) % NZ


def kernel(
    gen_hbm, freq_hbm, widths_hbm, ridge_hbm, dir_hbm, near_hbm, far_hbm,
    freq_ref, widths_ref, ridge_ref, dir_ref, gbuf, std, own, psend, precv, rsend, rrecv, shared, acc, xsend, xrecv, ysend, near, bounds,
    isem, gsem, psend_sem, precv_sem, rsend_sem, rrecv_sem, asend_sem, arecv_sem, ssend_sem, srecv_sem,
    xsend_sem, xrecv_sem, ysend_sem, yrecv_sem, out_sem, known_sem,
):
    half, rows = dir_ref.shape[1:]
    rhs = NCORE * half
    group = gbuf.shape[2]
    variants = NX * NH * NZ * group
    ci, si = lax.axis_index("chrom"), lax.axis_index("samp")
    z, y, core = si // (NY * NCORE), lax.rem(si // NCORE, NY), lax.rem(si, NCORE)
    x, yh = ci // NH, lax.rem(ci, NH)

    def samp_at(off, q):
        return (ci, (lax.rem(z + off, NZ) * NY + q) * NCORE + core)

    def samp_dev(off, dq):
        return samp_at(off, lax.rem(y + dq, NY))

    partner = (ci, si + 1 - 2 * core)

    def chrom_dev(dx, dh, dc=0):
        other = si + dc * (1 - 2 * core)
        return (lax.rem(x + dx, NX) * NH + lax.rem(yh + dh, NH), other)

    def lane_group(off):
        return lax.rem(z + off, NZ)

    def gcopy(i):
        lanes = pl.ds(pl.multiple_of(lane_group(far_first(i)) * group, 128), group)
        return pltpu.make_async_copy(gen_hbm.at[:, lanes], gbuf.at[i], gsem.at[i])

    def start_gcopy(i, _):
        gcopy(i).start()
        return 0

    small = [
        pltpu.make_async_copy(src, dst, isem.at[k])
        for k, (src, dst) in enumerate(
            (
                (dir_hbm, dir_ref), (freq_hbm, freq_ref),
                (widths_hbm, widths_ref), (ridge_hbm, ridge_ref),
            )
        )
    ]
    for copy in small:
        copy.start()
    loop(0, NZ, start_gcopy, 0)

    barrier = pltpu.get_barrier_semaphore()
    greeted = [samp_dev(off, dq) for off in (2, 6, 1, 7, 0) for dq in (2, 3, 1, 0) if off or dq]
    greeted += [chrom_dev(0, 1)]
    greeted += [chrom_dev(dx, 0, dc) for dx in (2, 1, 3, 0) for dc in range(NCORE) if dx or dc]
    for device in greeted:
        pl.semaphore_signal(barrier, inc=1, device_id=device, device_id_type=MESH)

    for copy in small:
        copy.wait()

    total = jnp.int32(0)
    for c in range(NX * NH):
        bounds[0, c] = total
        total = total + widths_ref[c]
        bounds[1, c] = total

    vector = dir_ref[...].reshape(rhs, rows).astype(BF16)

    def first_products(i, _):
        gcopy(i).wait()
        lg = lane_group(far_first(i))
        freq = freq_ref[:, pl.ds(pl.multiple_of(lg * group, 128), group)]
        doubled = 2.0 * freq
        scale = lax.rsqrt(doubled * (1.0 - freq))
        block = ((gbuf[i].astype(F32) - doubled) * scale).astype(BF16)
        std[lg, core] = block
        value = jnp.dot(vector, block, preferred_element_type=F32)
        own[i] = value
        psend[i] = value.astype(BF16)
        return 0

    loop(0, NZ, first_products, 0)

    pl.semaphore_wait(barrier, len(greeted))
    for off in (2, NZ - 2):
        pl.semaphore_signal(known_sem, inc=1, device_id=samp_dev(off, 0), device_id_type=MESH)

    def pair_copy(i):
        return pltpu.make_async_remote_copy(
            src_ref=psend.at[i, pl.ds(pl.multiple_of((1 - core) * half, half), half)],
            dst_ref=precv.at[i],
            send_sem=psend_sem.at[i], recv_sem=precv_sem.at[i],
            device_id=partner, device_id_type=MESH,
        )

    def pair_start(i, _):
        pair_copy(i).start()
        return 0

    loop(0, NZ, pair_start, 0)

    def scatter_copy(i, off, dq):
        return pltpu.make_async_remote_copy(
            src_ref=rsend.at[i, lax.rem(y + dq, NY)], dst_ref=rrecv.at[off, dq],
            send_sem=rsend_sem, recv_sem=rrecv_sem.at[off],
            device_id=samp_dev(off, dq), device_id_type=MESH,
        )

    def pair_sum(i):
        pair_copy(i).wait()
        mine = pl.multiple_of(core * half, half)
        value = own[i, pl.ds(mine, half), :] + precv[i].astype(F32)
        rsend[i] = value.astype(BF16).reshape(NY, half // NY, group)

    pair_sum(0)
    pl.semaphore_wait(known_sem, 2)

    def scatter(i, _):
        if i:
            pair_sum(i)
        off = far_first(i)
        for dq in (2, 3, 1, 0):
            scatter_copy(i, off, dq).start()
        return 0

    loop(0, NZ - 1, scatter, 0)
    pair_sum(NZ - 1)
    for dq in range(1, NY):
        scatter_copy(NZ - 1, 0, dq).start()

    def std_copy(i):
        lg = lane_group(near_first(i))
        return pltpu.make_async_remote_copy(
            src_ref=std.at[lg, core], dst_ref=std.at[lg, core],
            send_sem=ssend_sem.at[i], recv_sem=srecv_sem.at[i],
            device_id=partner, device_id_type=MESH,
        )

    for i in range(NZ):
        std_copy(i).start()

    block = rsend[NZ - 1, y].astype(F32)
    for off in (0, 1, 7, 2, 6, 3, 5, 4):
        part = rrecv.at[off, pl.ds(1, NY - 1)] if off == 0 else rrecv.at[off]
        pltpu.make_async_copy(part, part, rrecv_sem.at[off]).wait()
        for dq in range(NY):
            if off or dq:
                block = block + rrecv[off, dq].astype(F32)
    shared[z, y] = block.astype(BF16)

    def gather_copy(off, dq):
        return pltpu.make_async_remote_copy(
            src_ref=shared.at[z, y], dst_ref=shared.at[z, y],
            send_sem=asend_sem, recv_sem=arecv_sem.at[off],
            device_id=samp_dev(off, dq), device_id_type=MESH,
        )

    def gather(i, _):
        for dq in (2, 3, 1, 0):
            gather_copy(far_first(i), dq).start()
        return 0

    loop(0, NZ - 1, gather, 0)
    for dq in range(1, NY):
        gather_copy(0, dq).start()

    order = [(dx, dh) for dh in (1, 0) for dx in (2, 1, 3, 0)]
    sections = [lax.rem(x + dx, NX) * NH + lax.rem(yh + dh, NH) for dx, dh in order]

    for i in range(NZ):
        std_copy(i).wait()
    for first, last in CHUNKS:
        left, right = [], []
        for i in range(first, last):
            off = near_first(i)
            lg = lane_group(NZ - off)
            part = rrecv.at[0, pl.ds(1, NY - 1)] if off == 0 else rrecv.at[0]
            pltpu.make_async_copy(part, part, arecv_sem.at[off]).wait()
            value = shared[lg].astype(F32).reshape(half, group)
            var = (ci * NZ + lg) * group + lax.broadcasted_iota(jnp.int32, (1, group), 1)
            pieces = []
            for c in sections:
                inside = (var >= bounds[0, c]) & (var < bounds[1, c])
                pieces.append((value * jnp.where(inside, 0.0, 1.0)).astype(BF16))
            left.append(jnp.concatenate(pieces, axis=0))
            right.append(std[lg].reshape(NCORE * rows, group))
        product = lax.dot_general(
            jnp.concatenate(left, axis=1), jnp.concatenate(right, axis=1),
            (((1,), (1,)), ((), ())), preferred_element_type=F32,
        )
        for dc in range(NCORE):
            part = product[:, dc * rows : (dc + 1) * rows]
            acc[dc] = part if first == 0 else acc[dc] + part

    def x_copy(j, dx, dc):
        return pltpu.make_async_remote_copy(
            src_ref=xsend.at[j, dc], dst_ref=xrecv.at[j, dc],
            send_sem=xsend_sem.at[j, dc], recv_sem=xrecv_sem.at[j, dc],
            device_id=chrom_dev(dx, 0, dc), device_id_type=MESH,
        )

    for j, (dx, dh) in enumerate(order):
        for dc in range(NCORE):
            if dx or dc:
                to = lax.rem(core + dc, NCORE)
                xsend[j, dc] = acc[to, j * half : (j + 1) * half, :].astype(BF16)
                x_copy(j, dx, dc).start()

    def x_sum(first, dc):
        last = first + NX - 1
        value = None if dc else acc[core, last * half : (last + 1) * half, :]
        for j in (range(first, last), (last, *range(first, last)))[dc]:
            x_copy(j, order[j][0], dc).wait()
            part = xrecv[j, dc].astype(F32)
            value = part if value is None else value + part
        return value

    def divisor(c):
        return (variants - widths_ref[c]).astype(F32)

    for dc in (1, 0):
        ysend[lax.rem(core + dc, NCORE)] = (
            x_sum(0, dc) / divisor(ci + 1 - 2 * yh)
        ).astype(BF16)
    y_copy = pltpu.make_async_remote_copy(
        src_ref=ysend, dst_ref=far_hbm, send_sem=ysend_sem, recv_sem=yrecv_sem,
        device_id=chrom_dev(0, 1), device_id_type=MESH,
    )
    y_copy.start()
    for dc in (1, 0):
        rows_of = lax.rem(core + dc, NCORE)
        near[rows_of] = ridge_ref[0, 0] * dir_ref[rows_of] + x_sum(NX, dc) / divisor(ci)
    out_copy = pltpu.make_async_copy(near, near_hbm, out_sem)
    out_copy.start()

    sent = rrecv.at[pl.ds(1, NZ - 1)]
    rest = rrecv.at[0, pl.ds(1, NY - 1)]
    for sem in (rsend_sem, asend_sem):
        pltpu.make_async_copy(sent, sent, sem).wait()
        pltpu.make_async_copy(rest, rest, sem).wait()
    out_copy.wait()
    y_copy.wait()


def on_device(genotypes, frequency, widths, ridge_term, direction):
    rows, local_vars = genotypes.shape
    rhs = direction.shape[1]
    group = local_vars // NZ
    half = rhs // NCORE
    piece = half // NY
    sections = NX * NH
    dma, regular = pltpu.SemaphoreType.DMA, pltpu.SemaphoreType.REGULAR
    vmem, smem = pltpu.VMEM, pltpu.SMEM
    near, far = pl.pallas_call(
        kernel,
        out_shape=[jax.ShapeDtypeStruct((NCORE, half, rows), t) for t in (F32, BF16)],
        in_specs=[pl.BlockSpec(memory_space=pltpu.HBM)] * 5,
        out_specs=[pl.BlockSpec(memory_space=pl.ANY)] * 2,
        scratch_shapes=[
            vmem((1, local_vars), F32),
            smem((sections,), jnp.int32),
            smem((1, 1), F32),
            vmem((NCORE, half, rows), F32),
            vmem((NZ, rows, group), jnp.int32),
            vmem((NZ, NCORE, rows, group), BF16),
            vmem((NZ, rhs, group), F32),
            vmem((NZ, rhs, group), BF16),
            vmem((NZ, half, group), BF16),
            vmem((NZ, NY, piece, group), BF16),
            vmem((NZ, NY, piece, group), BF16),
            vmem((NZ, NY, piece, group), BF16),
            vmem((NCORE, sections * half, rows), F32),
            vmem((sections, NCORE, half, rows), BF16),
            vmem((sections, NCORE, half, rows), BF16),
            vmem((NCORE, half, rows), BF16),
            vmem((NCORE, half, rows), F32),
            smem((2, sections), jnp.int32),
            dma((4,)), dma((NZ,)), dma((NZ,)), dma((NZ,)),
            dma, dma((NZ,)), dma, dma((NZ,)), dma((NZ,)), dma((NZ,)),
            dma((sections, NCORE)), dma((sections, NCORE)), dma, dma, dma, regular,
        ],
        compiler_params=pltpu.CompilerParams(collective_id=0, has_side_effects=True),
        name="loco",
    )(
        genotypes, frequency.reshape(1, local_vars), widths, ridge_term.reshape(1, 1),
        direction.T.reshape(NCORE, half, rows),
    )
    out = (near + far.astype(F32)).reshape(rhs, rows)
    return out.T[None]


def solution(mesh):
    return jax.shard_map(
        on_device,
        mesh=mesh,
        in_specs=(P("samp", "chrom"), P("chrom"), P(), P(), P("samp", None)),
        out_specs=P("chrom", "samp", None),
        check_vma=False,
    )
```

```python
import jax
import jax.numpy as jnp
from jax import lax
from jax.experimental import pallas as pl
from jax.experimental.pallas import tpu as pltpu
from jax.sharding import PartitionSpec as P

MESH = pl.DeviceIdType.MESH
NZ, NY, NCORE = 8, 4, 2
NX, NH = 4, 2
CHUNKS = ((0, 8),)
BF16, F32 = jnp.bfloat16, jnp.float32


def loop(start, stop, body, carry):
    for i in range(start, stop):
        body(i, carry)


def far_first(i):
    half = NZ // 2
    return (half + (i + 1) // 2 if i % 2 else half - i // 2) % NZ


def near_first(i):
    return ((i + 1) // 2 if i % 2 else NZ - i // 2) % NZ


def kernel(
    gen_hbm, freq_hbm, widths_hbm, ridge_hbm, dir_hbm, near_hbm, far_hbm,
    freq_ref, widths_ref, ridge_ref, dir_ref, gbuf, std, own, psend, precv, rsend, rrecv, shared, acc, xsend, xrecv, ysend, near, bounds,
    isem, gsem, psend_sem, precv_sem, rsend_sem, rrecv_sem, asend_sem, arecv_sem, ssend_sem, srecv_sem,
    xsend_sem, xrecv_sem, ysend_sem, yrecv_sem, out_sem, known_sem,
):
    half, rows = dir_ref.shape[1:]
    rhs = NCORE * half
    group = gbuf.shape[2]
    variants = NX * NH * NZ * group
    ci, si = lax.axis_index("chrom"), lax.axis_index("samp")
    z, y, core = si // (NY * NCORE), lax.rem(si // NCORE, NY), lax.rem(si, NCORE)
    x, yh = ci // NH, lax.rem(ci, NH)

    def samp_at(off, q):
        return (ci, (lax.rem(z + off, NZ) * NY + q) * NCORE + core)

    def samp_dev(off, dq):
        return samp_at(off, lax.rem(y + dq, NY))

    partner = (ci, si + 1 - 2 * core)

    def chrom_dev(dx, dh, dc=0):
        other = si + dc * (1 - 2 * core)
        return (lax.rem(x + dx, NX) * NH + lax.rem(yh + dh, NH), other)

    def lane_group(off):
        return lax.rem(z + off, NZ)

    def gcopy(i):
        lanes = pl.ds(pl.multiple_of(lane_group(far_first(i)) * group, 128), group)
        return pltpu.make_async_copy(gen_hbm.at[:, lanes], gbuf.at[i], gsem.at[i])

    def start_gcopy(i, _):
        gcopy(i).start()
        return 0

    small = [
        pltpu.make_async_copy(src, dst, isem.at[k])
        for k, (src, dst) in enumerate(
            (
                (dir_hbm, dir_ref), (freq_hbm, freq_ref),
                (widths_hbm, widths_ref), (ridge_hbm, ridge_ref),
            )
        )
    ]
    for copy in small:
        copy.start()
    loop(0, NZ, start_gcopy, 0)

    barrier = pltpu.get_barrier_semaphore()
    greeted = [samp_dev(off, dq) for off in (2, 6, 1, 7, 0) for dq in (2, 3, 1, 0) if off or dq]
    greeted += [chrom_dev(0, 1)]
    greeted += [chrom_dev(dx, 0, dc) for dx in (2, 1, 3, 0) for dc in range(NCORE) if dx or dc]
    for device in greeted:
        pl.semaphore_signal(barrier, inc=1, device_id=device, device_id_type=MESH)

    for copy in small:
        copy.wait()

    total = jnp.int32(0)
    for c in range(NX * NH):
        bounds[0, c] = total
        total = total + widths_ref[c]
        bounds[1, c] = total

    vector = dir_ref[...].reshape(rhs, rows).astype(BF16)

    def first_products(i, _):
        gcopy(i).wait()
        lg = lane_group(far_first(i))
        freq = freq_ref[:, pl.ds(pl.multiple_of(lg * group, 128), group)]
        doubled = 2.0 * freq
        scale = lax.rsqrt(doubled * (1.0 - freq))
        block = ((gbuf[i].astype(F32) - doubled) * scale).astype(BF16)
        std[lg, core] = block
        value = jnp.dot(vector, block, preferred_element_type=F32)
        own[i] = value
        psend[i] = value.astype(BF16)
        return 0

    loop(0, NZ, first_products, 0)

    pl.semaphore_wait(barrier, len(greeted))
    for off in (2, NZ - 2):
        pl.semaphore_signal(known_sem, inc=1, device_id=samp_dev(off, 0), device_id_type=MESH)

    def pair_copy(i):
        return pltpu.make_async_remote_copy(
            src_ref=psend.at[i, pl.ds(pl.multiple_of((1 - core) * half, half), half)],
            dst_ref=precv.at[i],
            send_sem=psend_sem.at[i], recv_sem=precv_sem.at[i],
            device_id=partner, device_id_type=MESH,
        )

    def pair_start(i, _):
        pair_copy(i).start()
        return 0

    loop(0, NZ, pair_start, 0)

    def scatter_copy(i, off, dq):
        return pltpu.make_async_remote_copy(
            src_ref=rsend.at[i, lax.rem(y + dq, NY)], dst_ref=rrecv.at[off, dq],
            send_sem=rsend_sem, recv_sem=rrecv_sem.at[off],
            device_id=samp_dev(off, dq), device_id_type=MESH,
        )

    def pair_sum(i):
        pair_copy(i).wait()
        mine = pl.multiple_of(core * half, half)
        value = own[i, pl.ds(mine, half), :] + precv[i].astype(F32)
        rsend[i] = value.astype(BF16).reshape(NY, half // NY, group)

    pair_sum(0)
    pl.semaphore_wait(known_sem, 2)

    def scatter(i, _):
        if i:
            pair_sum(i)
        off = far_first(i)
        for dq in (2, 3, 1, 0):
            scatter_copy(i, off, dq).start()
        return 0

    loop(0, NZ - 1, scatter, 0)
    pair_sum(NZ - 1)
    for dq in range(1, NY):
        scatter_copy(NZ - 1, 0, dq).start()

    def std_copy(i):
        lg = lane_group(near_first(i))
        return pltpu.make_async_remote_copy(
            src_ref=std.at[lg, core], dst_ref=std.at[lg, core],
            send_sem=ssend_sem.at[i], recv_sem=srecv_sem.at[i],
            device_id=partner, device_id_type=MESH,
        )

    for i in range(NZ):
        std_copy(i).start()

    block = rsend[NZ - 1, y].astype(F32)
    for off in (0, 1, 7, 2, 6, 3, 5, 4):
        part = rrecv.at[off, pl.ds(1, NY - 1)] if off == 0 else rrecv.at[off]
        pltpu.make_async_copy(part, part, rrecv_sem.at[off]).wait()
        for dq in range(NY):
            if off or dq:
                block = block + rrecv[off, dq].astype(F32)
    shared[z, y] = block.astype(BF16)

    def gather_copy(off, dq):
        return pltpu.make_async_remote_copy(
            src_ref=shared.at[z, y], dst_ref=shared.at[z, y],
            send_sem=asend_sem, recv_sem=arecv_sem.at[off],
            device_id=samp_dev(off, dq), device_id_type=MESH,
        )

    def gather(i, _):
        for dq in (2, 3, 1, 0):
            gather_copy(far_first(i), dq).start()
        return 0

    loop(0, NZ - 1, gather, 0)
    for dq in range(1, NY):
        gather_copy(0, dq).start()

    order = [(dx, dh) for dh in (1, 0) for dx in (2, 1, 3, 0)]
    sections = [lax.rem(x + dx, NX) * NH + lax.rem(yh + dh, NH) for dx, dh in order]

    for i in range(NZ):
        std_copy(i).wait()
    for first, last in CHUNKS:
        left, right = [], []
        for i in range(first, last):
            off = near_first(i)
            lg = lane_group(NZ - off)
            part = rrecv.at[0, pl.ds(1, NY - 1)] if off == 0 else rrecv.at[0]
            pltpu.make_async_copy(part, part, arecv_sem.at[off]).wait()
            value = shared[lg].astype(F32).reshape(half, group)
            var = (ci * NZ + lg) * group + lax.broadcasted_iota(jnp.int32, (1, group), 1)
            pieces = []
            for c in sections:
                inside = (var >= bounds[0, c]) & (var < bounds[1, c])
                pieces.append((value * jnp.where(inside, 0.0, 1.0)).astype(BF16))
            left.append(jnp.concatenate(pieces, axis=0))
            right.append(std[lg].reshape(NCORE * rows, group))
        product = lax.dot_general(
            jnp.concatenate(left, axis=1), jnp.concatenate(right, axis=1),
            (((1,), (1,)), ((), ())), preferred_element_type=F32,
        )
        for dc in range(NCORE):
            part = product[:, dc * rows : (dc + 1) * rows]
            acc[dc] = part if first == 0 else acc[dc] + part

    def x_copy(j, dx, dc):
        return pltpu.make_async_remote_copy(
            src_ref=xsend.at[j, dc], dst_ref=xrecv.at[j, dc],
            send_sem=xsend_sem.at[j, dc], recv_sem=xrecv_sem.at[j, dc],
            device_id=chrom_dev(dx, 0, dc), device_id_type=MESH,
        )

    for j, (dx, dh) in enumerate(order):
        for dc in range(NCORE):
            if dx or dc:
                to = lax.rem(core + dc, NCORE)
                xsend[j, dc] = acc[to, j * half : (j + 1) * half, :].astype(BF16)
                x_copy(j, dx, dc).start()

    def x_sum(first, dc):
        last = first + NX - 1
        value = None if dc else acc[core, last * half : (last + 1) * half, :]
        for j in (range(first, last), (last, *range(first, last)))[dc]:
            x_copy(j, order[j][0], dc).wait()
            part = xrecv[j, dc].astype(F32)
            value = part if value is None else value + part
        return value

    def divisor(c):
        return (variants - widths_ref[c]).astype(F32)

    def y_copy(dc):
        rows_of = lax.rem(core + dc, NCORE)
        return pltpu.make_async_remote_copy(
            src_ref=ysend.at[rows_of], dst_ref=far_hbm.at[rows_of],
            send_sem=ysend_sem.at[dc], recv_sem=yrecv_sem.at[dc],
            device_id=chrom_dev(0, 1), device_id_type=MESH,
        )

    for dc in (0, 1):
        ysend[lax.rem(core + dc, NCORE)] = (
            x_sum(0, dc) / divisor(ci + 1 - 2 * yh)
        ).astype(BF16)
        y_copy(dc).start()
    for dc in (1, 0):
        rows_of = lax.rem(core + dc, NCORE)
        near[rows_of] = ridge_ref[0, 0] * dir_ref[rows_of] + x_sum(NX, dc) / divisor(ci)
    out_copy = pltpu.make_async_copy(near, near_hbm, out_sem)
    out_copy.start()

    sent = rrecv.at[pl.ds(1, NZ - 1)]
    rest = rrecv.at[0, pl.ds(1, NY - 1)]
    for sem in (rsend_sem, asend_sem):
        pltpu.make_async_copy(sent, sent, sem).wait()
        pltpu.make_async_copy(rest, rest, sem).wait()
    out_copy.wait()
    for dc in range(NCORE):
        y_copy(dc).wait()


def on_device(genotypes, frequency, widths, ridge_term, direction):
    rows, local_vars = genotypes.shape
    rhs = direction.shape[1]
    group = local_vars // NZ
    half = rhs // NCORE
    piece = half // NY
    sections = NX * NH
    dma, regular = pltpu.SemaphoreType.DMA, pltpu.SemaphoreType.REGULAR
    vmem, smem = pltpu.VMEM, pltpu.SMEM
    near, far = pl.pallas_call(
        kernel,
        out_shape=[jax.ShapeDtypeStruct((NCORE, half, rows), t) for t in (F32, BF16)],
        in_specs=[pl.BlockSpec(memory_space=pltpu.HBM)] * 5,
        out_specs=[pl.BlockSpec(memory_space=pl.ANY)] * 2,
        scratch_shapes=[
            vmem((1, local_vars), F32),
            smem((sections,), jnp.int32),
            smem((1, 1), F32),
            vmem((NCORE, half, rows), F32),
            vmem((NZ, rows, group), jnp.int32),
            vmem((NZ, NCORE, rows, group), BF16),
            vmem((NZ, rhs, group), F32),
            vmem((NZ, rhs, group), BF16),
            vmem((NZ, half, group), BF16),
            vmem((NZ, NY, piece, group), BF16),
            vmem((NZ, NY, piece, group), BF16),
            vmem((NZ, NY, piece, group), BF16),
            vmem((NCORE, sections * half, rows), F32),
            vmem((sections, NCORE, half, rows), BF16),
            vmem((sections, NCORE, half, rows), BF16),
            vmem((NCORE, half, rows), BF16),
            vmem((NCORE, half, rows), F32),
            smem((2, sections), jnp.int32),
            dma((4,)), dma((NZ,)), dma((NZ,)), dma((NZ,)),
            dma, dma((NZ,)), dma, dma((NZ,)), dma((NZ,)), dma((NZ,)),
            dma((sections, NCORE)), dma((sections, NCORE)),
            dma((NCORE,)), dma((NCORE,)), dma, regular,
        ],
        compiler_params=pltpu.CompilerParams(collective_id=0, has_side_effects=True),
        name="loco",
    )(
        genotypes, frequency.reshape(1, local_vars), widths, ridge_term.reshape(1, 1),
        direction.T.reshape(NCORE, half, rows),
    )
    out = (near + far.astype(F32)).reshape(rhs, rows)
    return out.T[None]


def solution(mesh):
    return jax.shard_map(
        on_device,
        mesh=mesh,
        in_specs=(P("samp", "chrom"), P("chrom"), P(), P(), P("samp", None)),
        out_specs=P("chrom", "samp", None),
        check_vma=False,
    )
```

```python
import jax
import jax.numpy as jnp
from jax import lax
from jax.experimental import pallas as pl
from jax.experimental.pallas import tpu as pltpu
from jax.sharding import PartitionSpec as P

MESH = pl.DeviceIdType.MESH
NZ, NY, NCORE = 8, 4, 2
NX, NH = 4, 2
CHUNKS = ((0, 8),)
BF16, F32 = jnp.bfloat16, jnp.float32


def loop(start, stop, body, carry):
    for i in range(start, stop):
        body(i, carry)


def far_first(i):
    return (4, 3, 5, 2, 6, 1, 7, 0)[i]


def near_first(i):
    return ((i + 1) // 2 if i % 2 else NZ - i // 2) % NZ


def kernel(
    gen_hbm, freq_hbm, widths_hbm, ridge_hbm, dir_hbm, near_hbm, far_hbm,
    freq_ref, widths_ref, ridge_ref, dir_ref, gbuf, std, own, psend, precv, rsend, rrecv, shared, acc, xsend, xrecv, ysend, near, bounds,
    isem, gsem, psend_sem, precv_sem, rsend_sem, rrecv_sem, asend_sem, arecv_sem, ssend_sem, srecv_sem,
    xsend_sem, xrecv_sem, ysend_sem, yrecv_sem, out_sem, known_sem,
):
    half, rows = dir_ref.shape[1:]
    rhs = NCORE * half
    group = gbuf.shape[2]
    variants = NX * NH * NZ * group
    ci, si = lax.axis_index("chrom"), lax.axis_index("samp")
    z, y, core = si // (NY * NCORE), lax.rem(si // NCORE, NY), lax.rem(si, NCORE)
    x, yh = ci // NH, lax.rem(ci, NH)

    def samp_at(off, q):
        return (ci, (lax.rem(z + off, NZ) * NY + q) * NCORE + core)

    def samp_dev(off, dq):
        return samp_at(off, lax.rem(y + dq, NY))

    partner = (ci, si + 1 - 2 * core)

    def chrom_dev(dx, dh, dc=0):
        other = si + dc * (1 - 2 * core)
        return (lax.rem(x + dx, NX) * NH + lax.rem(yh + dh, NH), other)

    def lane_group(off):
        return lax.rem(z + off, NZ)

    def gcopy(i):
        lanes = pl.ds(pl.multiple_of(lane_group(far_first(i)) * group, 128), group)
        return pltpu.make_async_copy(gen_hbm.at[:, lanes], gbuf.at[i], gsem.at[i])

    def start_gcopy(i, _):
        gcopy(i).start()
        return 0

    small = [
        pltpu.make_async_copy(src, dst, isem.at[k])
        for k, (src, dst) in enumerate(
            (
                (dir_hbm, dir_ref), (freq_hbm, freq_ref),
                (widths_hbm, widths_ref), (ridge_hbm, ridge_ref),
            )
        )
    ]
    for copy in small:
        copy.start()
    loop(0, NZ, start_gcopy, 0)

    barrier = pltpu.get_barrier_semaphore()
    greeted = [samp_dev(off, dq) for off in (2, 6, 1, 7, 0) for dq in (2, 3, 1, 0) if off or dq]
    greeted += [chrom_dev(0, 1)]
    greeted += [chrom_dev(dx, 0, dc) for dx in (2, 1, 3, 0) for dc in range(NCORE) if dx or dc]
    for device in greeted:
        pl.semaphore_signal(barrier, inc=1, device_id=device, device_id_type=MESH)

    for copy in small:
        copy.wait()

    total = jnp.int32(0)
    for c in range(NX * NH):
        bounds[0, c] = total
        total = total + widths_ref[c]
        bounds[1, c] = total

    vector = dir_ref[...].reshape(rhs, rows).astype(BF16)

    def first_products(i, _):
        gcopy(i).wait()
        lg = lane_group(far_first(i))
        freq = freq_ref[:, pl.ds(pl.multiple_of(lg * group, 128), group)]
        doubled = 2.0 * freq
        scale = lax.rsqrt(doubled * (1.0 - freq))
        block = ((gbuf[i].astype(F32) - doubled) * scale).astype(BF16)
        std[lg, core] = block
        value = jnp.dot(vector, block, preferred_element_type=F32)
        own[i] = value
        psend[i] = value.astype(BF16)
        return 0

    loop(0, NZ, first_products, 0)

    pl.semaphore_wait(barrier, len(greeted))
    for off in (2, NZ - 2):
        pl.semaphore_signal(known_sem, inc=1, device_id=samp_dev(off, 0), device_id_type=MESH)

    def pair_copy(i):
        return pltpu.make_async_remote_copy(
            src_ref=psend.at[i, pl.ds(pl.multiple_of((1 - core) * half, half), half)],
            dst_ref=precv.at[i],
            send_sem=psend_sem.at[i], recv_sem=precv_sem.at[i],
            device_id=partner, device_id_type=MESH,
        )

    def pair_start(i, _):
        pair_copy(i).start()
        return 0

    loop(0, NZ, pair_start, 0)

    def scatter_copy(i, off, dq):
        return pltpu.make_async_remote_copy(
            src_ref=rsend.at[i, lax.rem(y + dq, NY)], dst_ref=rrecv.at[off, dq],
            send_sem=rsend_sem, recv_sem=rrecv_sem.at[off],
            device_id=samp_dev(off, dq), device_id_type=MESH,
        )

    def pair_sum(i):
        pair_copy(i).wait()
        mine = pl.multiple_of(core * half, half)
        value = own[i, pl.ds(mine, half), :] + precv[i].astype(F32)
        rsend[i] = value.astype(BF16).reshape(NY, half // NY, group)

    pair_sum(0)
    pl.semaphore_wait(known_sem, 2)

    def scatter(i, _):
        if i:
            pair_sum(i)
        off = far_first(i)
        for dq in (2, 3, 1, 0):
            scatter_copy(i, off, dq).start()
        return 0

    loop(0, NZ - 1, scatter, 0)
    pair_sum(NZ - 1)
    for dq in range(1, NY):
        scatter_copy(NZ - 1, 0, dq).start()

    def std_copy(i):
        lg = lane_group(near_first(i))
        return pltpu.make_async_remote_copy(
            src_ref=std.at[lg, core], dst_ref=std.at[lg, core],
            send_sem=ssend_sem.at[i], recv_sem=srecv_sem.at[i],
            device_id=partner, device_id_type=MESH,
        )

    for i in range(NZ):
        std_copy(i).start()

    block = rsend[NZ - 1, y].astype(F32)
    for off in (0, 1, 7, 2, 6, 3, 5, 4):
        part = rrecv.at[off, pl.ds(1, NY - 1)] if off == 0 else rrecv.at[off]
        pltpu.make_async_copy(part, part, rrecv_sem.at[off]).wait()
        for dq in range(NY):
            if off or dq:
                block = block + rrecv[off, dq].astype(F32)
    shared[z, y] = block.astype(BF16)

    def gather_copy(off, dq):
        return pltpu.make_async_remote_copy(
            src_ref=shared.at[z, y], dst_ref=shared.at[z, y],
            send_sem=asend_sem, recv_sem=arecv_sem.at[off],
            device_id=samp_dev(off, dq), device_id_type=MESH,
        )

    def gather(i, _):
        for dq in (2, 3, 1, 0):
            gather_copy(far_first(i), dq).start()
        return 0

    loop(0, NZ - 1, gather, 0)
    for dq in range(1, NY):
        gather_copy(0, dq).start()

    order = [(dx, dh) for dh in (1, 0) for dx in (2, 1, 3, 0)]
    sections = [lax.rem(x + dx, NX) * NH + lax.rem(yh + dh, NH) for dx, dh in order]

    for i in range(NZ):
        std_copy(i).wait()
    for first, last in CHUNKS:
        left, right = [], []
        for i in range(first, last):
            off = near_first(i)
            lg = lane_group(NZ - off)
            part = rrecv.at[0, pl.ds(1, NY - 1)] if off == 0 else rrecv.at[0]
            pltpu.make_async_copy(part, part, arecv_sem.at[off]).wait()
            value = shared[lg].astype(F32).reshape(half, group)
            var = (ci * NZ + lg) * group + lax.broadcasted_iota(jnp.int32, (1, group), 1)
            pieces = []
            for c in sections:
                inside = (var >= bounds[0, c]) & (var < bounds[1, c])
                pieces.append((value * jnp.where(inside, 0.0, 1.0)).astype(BF16))
            left.append(jnp.concatenate(pieces, axis=0))
            right.append(std[lg].reshape(NCORE * rows, group))
        product = lax.dot_general(
            jnp.concatenate(left, axis=1), jnp.concatenate(right, axis=1),
            (((1,), (1,)), ((), ())), preferred_element_type=F32,
        )
        for dc in range(NCORE):
            part = product[:, dc * rows : (dc + 1) * rows]
            acc[dc] = part if first == 0 else acc[dc] + part

    def x_copy(j, dx, dc):
        return pltpu.make_async_remote_copy(
            src_ref=xsend.at[j, dc], dst_ref=xrecv.at[j, dc],
            send_sem=xsend_sem.at[j, dc], recv_sem=xrecv_sem.at[j, dc],
            device_id=chrom_dev(dx, 0, dc), device_id_type=MESH,
        )

    for j, (dx, dh) in enumerate(order):
        for dc in range(NCORE):
            if dx or dc:
                to = lax.rem(core + dc, NCORE)
                xsend[j, dc] = acc[to, j * half : (j + 1) * half, :].astype(BF16)
                x_copy(j, dx, dc).start()

    def x_sum(first, dc):
        last = first + NX - 1
        value = None if dc else acc[core, last * half : (last + 1) * half, :]
        for j in (range(first, last), (last, *range(first, last)))[dc]:
            x_copy(j, order[j][0], dc).wait()
            part = xrecv[j, dc].astype(F32)
            value = part if value is None else value + part
        return value

    def divisor(c):
        return (variants - widths_ref[c]).astype(F32)

    def y_copy(dc):
        rows_of = lax.rem(core + dc, NCORE)
        return pltpu.make_async_remote_copy(
            src_ref=ysend.at[rows_of], dst_ref=far_hbm.at[rows_of],
            send_sem=ysend_sem.at[dc], recv_sem=yrecv_sem.at[dc],
            device_id=chrom_dev(0, 1), device_id_type=MESH,
        )

    for dc in (0, 1):
        ysend[lax.rem(core + dc, NCORE)] = (
            x_sum(0, dc) / divisor(ci + 1 - 2 * yh)
        ).astype(BF16)
        y_copy(dc).start()
    for dc in (1, 0):
        rows_of = lax.rem(core + dc, NCORE)
        near[rows_of] = ridge_ref[0, 0] * dir_ref[rows_of] + x_sum(NX, dc) / divisor(ci)
    out_copy = pltpu.make_async_copy(near, near_hbm, out_sem)
    out_copy.start()

    sent = rrecv.at[pl.ds(1, NZ - 1)]
    rest = rrecv.at[0, pl.ds(1, NY - 1)]
    for sem in (rsend_sem, asend_sem):
        pltpu.make_async_copy(sent, sent, sem).wait()
        pltpu.make_async_copy(rest, rest, sem).wait()
    out_copy.wait()
    for dc in range(NCORE):
        y_copy(dc).wait()


def on_device(genotypes, frequency, widths, ridge_term, direction):
    rows, local_vars = genotypes.shape
    rhs = direction.shape[1]
    group = local_vars // NZ
    half = rhs // NCORE
    piece = half // NY
    sections = NX * NH
    dma, regular = pltpu.SemaphoreType.DMA, pltpu.SemaphoreType.REGULAR
    vmem, smem = pltpu.VMEM, pltpu.SMEM
    near, far = pl.pallas_call(
        kernel,
        out_shape=[jax.ShapeDtypeStruct((NCORE, half, rows), t) for t in (F32, BF16)],
        in_specs=[pl.BlockSpec(memory_space=pltpu.HBM)] * 5,
        out_specs=[pl.BlockSpec(memory_space=pl.ANY)] * 2,
        scratch_shapes=[
            vmem((1, local_vars), F32),
            smem((sections,), jnp.int32),
            smem((1, 1), F32),
            vmem((NCORE, half, rows), F32),
            vmem((NZ, rows, group), jnp.int32),
            vmem((NZ, NCORE, rows, group), BF16),
            vmem((NZ, rhs, group), F32),
            vmem((NZ, rhs, group), BF16),
            vmem((NZ, half, group), BF16),
            vmem((NZ, NY, piece, group), BF16),
            vmem((NZ, NY, piece, group), BF16),
            vmem((NZ, NY, piece, group), BF16),
            vmem((NCORE, sections * half, rows), F32),
            vmem((sections, NCORE, half, rows), BF16),
            vmem((sections, NCORE, half, rows), BF16),
            vmem((NCORE, half, rows), BF16),
            vmem((NCORE, half, rows), F32),
            smem((2, sections), jnp.int32),
            dma((4,)), dma((NZ,)), dma((NZ,)), dma((NZ,)),
            dma, dma((NZ,)), dma, dma((NZ,)), dma((NZ,)), dma((NZ,)),
            dma((sections, NCORE)), dma((sections, NCORE)),
            dma((NCORE,)), dma((NCORE,)), dma, regular,
        ],
        compiler_params=pltpu.CompilerParams(collective_id=0, has_side_effects=True),
        name="loco",
    )(
        genotypes, frequency.reshape(1, local_vars), widths, ridge_term.reshape(1, 1),
        direction.T.reshape(NCORE, half, rows),
    )
    out = (near + far.astype(F32)).reshape(rhs, rows)
    return out.T[None]


def solution(mesh):
    return jax.shard_map(
        on_device,
        mesh=mesh,
        in_specs=(P("samp", "chrom"), P("chrom"), P(), P(), P("samp", None)),
        out_specs=P("chrom", "samp", None),
        check_vma=False,
    )
```
